128 devices in a mesh: wide: 16 (over y_lo, z, core), narrow: 8 (over x, y_hi).
Axes of the slice: x: 4, y: 4 (y_hi: 2, y_lo: 2; y = y_hi * 2 + y_lo), z: 4, core: 2. Of those that a mesh axis runs over, the one named last changes fastest.
Arguments:
- scalar_field: float32 [256, 512, 2048], P('wide', 'narrow'), may hold values from -6 to 6
- depth_rank: int32 [16], replicated, may hold values from 0 to 15, each once
- transfer: float32 [2, 3], replicated, may hold values from -2 to 2
- light_dir: float32 [3], replicated, may hold values from -1 to 1
Outputs:
- final_image: float32 [3, 512, 2048], P(None, 'narrow')
The draws below stay inside these ranges and needn't reach their ends.
Inputs may be any that keep to these rules, and one draw needn't show every extreme that they name: `depth_rank`: every rank 0 to 15 appears exactly once.
All inputs are finite; a program needn't handle non-finite values.
Results may differ from the reference program's by a relative error of at most 0.000067.
Values sent between devices are 32-bit elements; how exact they have to be, the bound alone decides.
A program may use at most 128 MiB of HBM per device.

```python
import jax
import jax.numpy as jnp
from jax import lax

COLS = 2048
PLANES = 16
ROWS = 512
NZ = 256
N_WIDE = 16


def level_of(stream_key, extent, pieces, least, high):
    loudness = 1.0
    for dim, shards_of in pieces:
        steps = jax.random.uniform(jax.random.fold_in(jax.random.fold_in(stream_key, 6), dim), (shards_of,), jnp.float32, least / len(pieces), high / len(pieces))
        loudness = loudness * jnp.repeat(jnp.exp(steps), extent[dim] // shards_of).reshape((-1,) + (1,) * (len(extent) - 1 - dim))
    return loudness


def centred(rng, extent, spread, bound, cuts=(), kind=jnp.bfloat16):
    entries = spread * jax.random.normal(rng, extent, jnp.float32)
    if cuts:
        entries = entries * level_of(rng, extent, cuts, -0.22, 0.18)
    return jnp.clip(entries, -bound, bound).astype(kind)


def setup_inputs(seed: int = 0) -> dict:
    keys = jax.random.split(jax.random.key(seed), 5)
    scalar_field = centred(keys[0], (NZ, ROWS, COLS), 1.0, 6.0, ((0, 16), (1, 8)), jnp.float32)
    depth_rank = jax.random.permutation(keys[1], N_WIDE).astype(jnp.int32)
    transfer = jnp.clip(jax.random.uniform(keys[2], (2, 3), jnp.float32, -2.0, 2.0), -2.0, 2.0)
    light_dir = jnp.clip(jax.random.uniform(keys[3], (3,), jnp.float32, -1.0, 1.0), -1.0, 1.0)
    return dict(scalar_field=scalar_field, depth_rank=depth_rank, transfer=transfer, light_dir=light_dir)


background = 0.25
optical_total = 2.0


def march_steps(volume, plane_total):
    return jax.nn.softplus(2.0 * volume) * (optical_total / plane_total)


def render(padded, optical_step, light_dir, transfer):
    volume = padded[:, 1:-1, :]
    shifted_up = jnp.concatenate([volume[:1], volume[:-1]], axis=0)
    shifted_down = jnp.concatenate([volume[1:], volume[-1:]], axis=0)
    slope_depth = (shifted_down - shifted_up) * 0.5
    slope_rows = (padded[:, 2:, :] - padded[:, :-2, :]) * 0.5
    zero_column = jnp.zeros_like(volume[:, :, :1])
    right_cells = jnp.concatenate([volume[:, :, 1:], zero_column], axis=2)
    left_cells = jnp.concatenate([zero_column, volume[:, :, :-1]], axis=2)
    slope_cols = (right_cells - left_cells) * 0.5
    shading = 0.5 + 0.5 * jnp.tanh(light_dir[0] * slope_depth + light_dir[1] * slope_rows + light_dir[2] * slope_cols)
    passed = jnp.cumsum(optical_step, axis=0) - optical_step
    weights = jnp.exp(-passed) * (1.0 - jnp.exp(-optical_step)) * shading
    colors = jax.nn.sigmoid(transfer[0][:, None, None, None] * volume[None] + transfer[1][:, None, None, None])
    return jnp.sum(weights[None] * colors, axis=1)


def reference(scalar_field, depth_rank, transfer, light_dir):
    bricks = scalar_field.reshape(N_WIDE, PLANES, ROWS, COLS)

    def one_brick(volume):
        padded = jnp.pad(volume, ((0, 0), (1, 1), (0, 0)))
        optical_step = march_steps(volume, NZ)
        return render(padded, optical_step, light_dir, transfer), jnp.sum(optical_step, axis=0)

    shaded_color, brick_depth = lax.map(one_brick, bricks)
    in_front = (depth_rank[None, :] < depth_rank[:, None]).astype(jnp.float32)
    front_depth = jnp.einsum("ab,byx->ayx", in_front, brick_depth, precision=lax.Precision.HIGHEST)
    total_depth = jnp.sum(brick_depth, axis=0)
    return jnp.sum(jnp.exp(-front_depth)[:, None] * shaded_color, axis=0) + background * jnp.exp(-total_depth)
```

```python
import functools
import math

import jax
import jax.numpy as jnp
from jax import lax
from jax.experimental import pallas as pl
from jax.experimental.pallas import tpu as pltpu
from jax.sharding import PartitionSpec as P

MESH = pl.DeviceIdType.MESH
BACKGROUND = 0.25
LOG2E = math.log2(math.e)
LAG = 2
PARTNERS = (
    (1, 2, 0), (1, 0, 0), (0, 2, 0), (0, 1, 0), (1, 1, 0), (0, 3, 0), (1, 3, 0),
    (1, 2, 1), (1, 0, 1), (0, 2, 1), (0, 1, 1), (1, 1, 1), (0, 3, 1), (1, 3, 1),
    (0, 0, 1),
)


def brick_cells(vol, tile, row, scale, light, trans):
    planes = vol.shape[0]
    lane = lax.broadcasted_iota(jnp.int32, (8, 128), 1)
    first, last = lane == 0, lane == 127
    zero = jnp.zeros((8, 128), jnp.float32)
    depth, through = zero, zero + 1.0
    acc = [zero] * 3
    value = vol[0, tile, pl.ds(row, 8), :]
    before = value
    for p in range(planes):
        after = vol[p + 1, tile, pl.ds(row, 8), :] if p + 1 < planes else value
        up = vol[p, tile, pl.ds(row - 1, 8), :]
        down = vol[p, tile, pl.ds(row + 1, 8), :]
        right = pltpu.roll(jnp.where(first, vol[p, tile + 1, pl.ds(row, 8), :], value), 127, 1)
        left = pltpu.roll(jnp.where(last, vol[p, tile - 1, pl.ds(row, 8), :], value), 1, 1)
        slope = light[0] * (after - before) + light[1] * (down - up) + light[2] * (right - left)
        depth = depth + jnp.log(1.0 + jnp.exp2(value * (2.0 * LOG2E)))
        beyond = jnp.exp2(depth * (-scale * LOG2E))
        weight = through - beyond
        through = beyond
        shaded = weight + weight * jnp.tanh(slope)
        den = [1.0 + jnp.exp2(trans[0][c] * value + trans[1][c]) for c in range(3)]
        den01 = den[0] * den[1]
        part = shaded / (den01 * den[2])
        part2 = part * den[2]
        acc[0] = acc[0] + part2 * den[1]
        acc[1] = acc[1] + part2 * den[0]
        acc[2] = acc[2] + part * den01
        before, value = value, after
    return acc, depth


def kernel(
    sizes, field, rank, transfer, light_dir, out,
    vol, send, recv, image, front,
    load_sem, halo_ssem, halo_rsem, send_sem, recv_sem, ag_ssem, ag_rsem, out_sem,
):
    wide, narrow, rows, scale = sizes
    blocks = wide
    chunks = rows // 8
    me = lax.axis_index("wide")
    row_part = lax.axis_index("narrow")
    y, z, core = me // 8, (me // 2) % 4, me % 2

    def device(dy, dz, dc):
        return ((y + dy) % 2) * 8 + ((z + dz) % 4) * 2 + (core + dc) % 2

    def column_block(dy, dz, dc):
        return ((core + dc) % 2) * 8 + ((z + dz) % 4) * 2 + (y + dy) % 2

    mine = column_block(0, 0, 0)

    barrier = pltpu.get_barrier_semaphore()
    for dy, dz, dc in PARTNERS:
        pl.semaphore_signal(barrier, inc=1, device_id=(device(dy, dz, dc), row_part), device_id_type=MESH)

    @pl.when(row_part > 0)
    def _():
        pl.semaphore_signal(barrier, inc=1, device_id=(me, row_part - 1), device_id_type=MESH)

    @pl.when(row_part < narrow - 1)
    def _():
        pl.semaphore_signal(barrier, inc=1, device_id=(me, row_part + 1), device_id_type=MESH)

    def load(k, part):
        lo, n = ((0, 24), (24, rows - 24))[part]
        return pltpu.make_async_copy(
            field.at[:, lo:lo + n, pl.ds(pl.multiple_of(k * 128, 128), 128)],
            vol.at[:, k + 1, 8 + lo:8 + lo + n, :],
            load_sem.at[part, k],
        )

    for part in range(2):
        def start_load(k, _, part=part):
            load(k, part).start()
            return 0
        lax.fori_loop(0, blocks, start_load, 0)

    def clear(p, _):
        vol[p, 0, 8:8 + rows, :] = jnp.zeros((rows, 128), jnp.float32)
        vol[p, blocks + 1, 8:8 + rows, :] = jnp.zeros((rows, 128), jnp.float32)
        return 0

    lax.fori_loop(0, vol.shape[0], clear, 0)

    def clear_row(at):
        def step(p, _):
            vol[p, 1:blocks + 1, at:at + 1, :] = jnp.zeros((blocks, 1, 128), jnp.float32)
            return 0
        lax.fori_loop(0, vol.shape[0], step, 0)

    @pl.when(row_part == 0)
    def _():
        clear_row(7)

    @pl.when(row_part == narrow - 1)
    def _():
        clear_row(8 + rows)

    for b in range(wide):
        for o in range(wide):
            front[b * wide + o] = jnp.where(rank[o] < rank[b], 1.0, 0.0)

    light = [0.5 * light_dir[i] for i in range(3)]
    trans = [[-LOG2E * transfer[i, c] for c in range(3)] for i in range(2)]

    def wait_load(part):
        lo, n = ((0, 24), (24, rows - 24))[part]
        for k in range(blocks):
            load(k, part).wait()

    def compute(chunk):
        row = 8 + 8 * chunk

        def step(k, _):
            acc, depth = brick_cells(vol, k + 1, row, scale, light, trans)
            for c in range(3):
                send[chunk, k, c] = acc[c] * 0.5
            send[chunk, k, 3] = depth * scale
            return 0

        lax.fori_loop(0, blocks, step, 0)

    def block_copy(chunk, dy, dz, dc):
        return pltpu.make_async_remote_copy(
            src_ref=send.at[chunk, column_block(dy, dz, dc)],
            dst_ref=recv.at[chunk, me],
            send_sem=send_sem.at[chunk],
            recv_sem=recv_sem.at[chunk],
            device_id=(device(dy, dz, dc), row_part),
            device_id_type=MESH,
        )

    def send_chunk(chunk):
        for partner in PARTNERS:
            block_copy(chunk, *partner).start()

    def all_of(chunk):
        part = recv.at[chunk, 0:wide - 1]
        return pltpu.make_async_remote_copy(
            src_ref=send.at[chunk, 0:wide - 1], dst_ref=part, send_sem=send_sem.at[chunk], recv_sem=recv_sem.at[chunk],
            device_id=(device(1, 0, 0), row_part), device_id_type=MESH,
        )

    def composite(chunk):
        recv[chunk, me] = send[chunk, mine]
        all_of(chunk).wait_recv()
        depths = [recv[chunk, b, 3] for b in range(wide)]
        total = depths[0]
        for b in range(1, wide):
            total = total + depths[b]
        back = BACKGROUND * jnp.exp(-total)
        acc = [back] * 3
        for b in range(wide):
            ahead = jnp.zeros((8, 128), jnp.float32)
            for o in range(wide):
                if o != b:
                    ahead = ahead + front[b * wide + o] * depths[o]
            seen = jnp.exp(-ahead)
            for c in range(3):
                acc[c] = acc[c] + seen * recv[chunk, b, c]
        for c in range(3):
            image[c, chunk * 8:chunk * 8 + 8, pl.ds(pl.multiple_of(mine * 128, 128), 128)] = acc[c]

    def tile(chunk, start, count):
        return image.at[:, chunk * 8:chunk * 8 + 8, pl.ds(pl.multiple_of(start * 128, 128), count * 128)]

    def gather_copy(chunk, slot, start, count, dy, dz, dc, got):
        def made(at):
            return pltpu.make_async_remote_copy(
                src_ref=tile(chunk, at, count), dst_ref=tile(chunk, at, count),
                send_sem=ag_ssem.at[chunk, slot], recv_sem=ag_rsem.at[chunk, slot],
                device_id=(device(dy, dz, dc), row_part), device_id_type=MESH,
            )
        return functools.partial(made, start), functools.partial(made, got)

    def pair(dz):
        return core * 8 + ((z + dz) % 4) * 2

    def stage1(chunk):
        return [gather_copy(chunk, 0, mine, 1, 1, 0, 0, column_block(1, 0, 0))]

    def stage2(chunk):
        return [
            gather_copy(chunk, 1, pair(0), 2, 0, 1, 0, pair(3)),
            gather_copy(chunk, 2, pair(0), 2, 0, 3, 0, pair(1)),
        ]

    def stage3(chunk):
        return [
            gather_copy(chunk, 3, pair(3), 1, 0, 1, 0, pair(2)),
            gather_copy(chunk, 4, pair(1) + 1, 1, 0, 3, 0, pair(2) + 1),
        ]

    def stage4(chunk):
        return [gather_copy(chunk, 5, core * 8, 8, 0, 0, 1, ((core + 1) % 2) * 8)]

    stages = (stage1, stage2, stage3, stage4)

    def begin(stage, chunk):
        for sent, _ in stages[stage](chunk):
            sent().start()

    def end(stage, chunk):
        for _, got in stages[stage](chunk):
            got().wait_recv()

    def write(chunk):
        return pltpu.make_async_copy(
            image.at[:, chunk * 8:chunk * 8 + 8, :], out.at[:, chunk * 8:chunk * 8 + 8, :], out_sem.at[chunk]
        )

    def halo_up():
        return pltpu.make_async_remote_copy(
            src_ref=vol.at[:, 1:blocks + 1, 8:9, :], dst_ref=vol.at[:, 1:blocks + 1, 8 + rows:9 + rows, :],
            send_sem=halo_ssem.at[0], recv_sem=halo_rsem.at[0],
            device_id=(me, row_part - 1), device_id_type=MESH,
        )

    def halo_down():
        return pltpu.make_async_remote_copy(
            src_ref=vol.at[:, 1:blocks + 1, 7 + rows:8 + rows, :], dst_ref=vol.at[:, 1:blocks + 1, 7:8, :],
            send_sem=halo_ssem.at[1], recv_sem=halo_rsem.at[1],
            device_id=(me, row_part + 1), device_id_type=MESH,
        )

    has_up, has_down = row_part > 0, row_part < narrow - 1
    order = list(range(1, chunks - 1)) + [0, chunks - 1]
    last = chunks + LAG + 4
    for step in range(last):
        if step == 0:
            wait_load(0)
        if step < chunks:
            chunk = order[step]
            if chunk == 0:
                @pl.when(has_up)
                def _():
                    halo_down().wait_recv()
            if chunk == chunks - 1:
                @pl.when(has_down)
                def _():
                    halo_up().wait_recv()
            compute(chunk)
        if step == 0:
            wait_load(1)
            pl.semaphore_wait(barrier, wide - 1 + has_up.astype(jnp.int32) + has_down.astype(jnp.int32))

            @pl.when(has_up)
            def _():
                halo_up().start()

            @pl.when(has_down)
            def _():
                halo_down().start()
        if step < chunks:
            send_chunk(order[step])
        for stage in range(4, -1, -1):
            at = step - LAG - stage
            if 0 <= at < chunks:
                chunk = order[at]
                if stage == 0:
                    composite(chunk)
                    begin(0, chunk)
                else:
                    end(stage - 1, chunk)
                    if stage < 4:
                        begin(stage, chunk)
                    else:
                        write(chunk).start()

    for chunk in range(chunks):
        all_of(chunk).wait_send()
        for stage in range(4):
            for sent, _ in stages[stage](chunk):
                sent().wait_send()
        write(chunk).wait()

    @pl.when(has_up)
    def _():
        halo_up().wait_send()

    @pl.when(has_down)
    def _():
        halo_down().wait_send()


def solution(mesh):
    wide, narrow = mesh.shape["wide"], mesh.shape["narrow"]

    def body(scalar_field, depth_rank, transfer, light_dir):
        planes, rows, columns = scalar_field.shape
        blocks = columns // 128
        chunks = rows // 8
        scale = 2.0 / (planes * wide)
        smem = pl.BlockSpec(memory_space=pltpu.SMEM)
        return pl.pallas_call(
            functools.partial(kernel, (wide, narrow, rows, scale)),
            out_shape=jax.ShapeDtypeStruct((3, rows, columns), jnp.float32),
            in_specs=[pl.BlockSpec(memory_space=pl.ANY), smem, smem, smem],
            out_specs=pl.BlockSpec(memory_space=pl.ANY),
            scratch_shapes=[
                pltpu.VMEM((planes, blocks + 2, rows + 16, 128), jnp.float32),
                pltpu.VMEM((chunks, blocks, 4, 8, 128), jnp.float32),
                pltpu.VMEM((chunks, wide, 4, 8, 128), jnp.float32),
                pltpu.VMEM((3, rows, columns), jnp.float32),
                pltpu.SMEM((wide * wide,), jnp.float32),
                pltpu.SemaphoreType.DMA((2, blocks)),
                pltpu.SemaphoreType.DMA((2,)),
                pltpu.SemaphoreType.DMA((2,)),
                pltpu.SemaphoreType.DMA((chunks,)),
                pltpu.SemaphoreType.DMA((chunks,)),
                pltpu.SemaphoreType.DMA((chunks, 6)),
                pltpu.SemaphoreType.DMA((chunks, 6)),
                pltpu.SemaphoreType.DMA((chunks,)),
            ],
            compiler_params=pltpu.CompilerParams(collective_id=0, has_side_effects=True),
        )(scalar_field, depth_rank, transfer, light_dir)

    return jax.shard_map(
        body,
        mesh=mesh,
        in_specs=(P("wide", "narrow", None), P(), P(), P()),
        out_specs=P(None, "narrow", None),
        check_vma=False,
    )
```

```python
import functools
import math

import jax
import jax.numpy as jnp
from jax import lax
from jax.experimental import pallas as pl
from jax.experimental.pallas import tpu as pltpu
from jax.sharding import PartitionSpec as P

MESH = pl.DeviceIdType.MESH
BACKGROUND = 0.25
LOG2E = math.log2(math.e)
LAG = 3
GAP = 3
DIRECT = 4
PARTNERS = (
    (1, 2, 0), (1, 0, 0), (0, 2, 0), (0, 1, 0), (1, 1, 0), (0, 3, 0), (1, 3, 0),
    (1, 2, 1), (1, 0, 1), (0, 2, 1), (0, 1, 1), (1, 1, 1), (0, 3, 1), (1, 3, 1),
    (0, 0, 1),
)


def brick_cells(vol, tile, row, scale, light, trans):
    planes = vol.shape[0]
    lane = lax.broadcasted_iota(jnp.int32, (8, 128), 1)
    first, last = lane == 0, lane == 127
    zero = jnp.zeros((8, 128), jnp.float32)
    depth, through = zero, zero + 1.0
    acc = [zero] * 3
    value = vol[0, tile, pl.ds(row, 8), :]
    before = value
    for p in range(planes):
        after = vol[p + 1, tile, pl.ds(row, 8), :] if p + 1 < planes else value
        up = vol[p, tile, pl.ds(row - 1, 8), :]
        down = vol[p, tile, pl.ds(row + 1, 8), :]
        right = pltpu.roll(jnp.where(first, vol[p, tile + 1, pl.ds(row, 8), :], value), 127, 1)
        left = pltpu.roll(jnp.where(last, vol[p, tile - 1, pl.ds(row, 8), :], value), 1, 1)
        slope = light[0] * (after - before) + light[1] * (down - up) + light[2] * (right - left)
        depth = depth + jnp.log(1.0 + jnp.exp2(value * (2.0 * LOG2E)))
        beyond = jnp.exp2(depth * (-scale * LOG2E))
        weight = through - beyond
        through = beyond
        shaded = weight + weight * jnp.tanh(slope)
        den = [1.0 + jnp.exp2(trans[0][c] * value + trans[1][c]) for c in range(3)]
        den01 = den[0] * den[1]
        part = shaded / (den01 * den[2])
        part2 = part * den[2]
        acc[0] = acc[0] + part2 * den[1]
        acc[1] = acc[1] + part2 * den[0]
        acc[2] = acc[2] + part * den01
        before, value = value, after
    return acc, depth


def kernel(
    sizes, field, rank, transfer, light_dir, out,
    vol, send, recv, image, front,
    load_sem, halo_ssem, halo_rsem, send_sem, recv_sem, ag_ssem, ag_rsem, out_sem,
):
    wide, narrow, rows, scale = sizes
    blocks = wide
    chunks = rows // 8
    me = lax.axis_index("wide")
    row_part = lax.axis_index("narrow")
    y, z, core = me // 8, (me // 2) % 4, me % 2

    def device(dy, dz, dc):
        return ((y + dy) % 2) * 8 + ((z + dz) % 4) * 2 + (core + dc) % 2

    def column_block(dy, dz, dc):
        return ((core + dc) % 2) * 8 + ((z + dz) % 4) * 2 + (y + dy) % 2

    mine = column_block(0, 0, 0)

    barrier = pltpu.get_barrier_semaphore()
    for dy, dz, dc in PARTNERS:
        pl.semaphore_signal(barrier, inc=1, device_id=(device(dy, dz, dc), row_part), device_id_type=MESH)

    @pl.when(row_part > 0)
    def _():
        pl.semaphore_signal(barrier, inc=1, device_id=(me, row_part - 1), device_id_type=MESH)

    @pl.when(row_part < narrow - 1)
    def _():
        pl.semaphore_signal(barrier, inc=1, device_id=(me, row_part + 1), device_id_type=MESH)

    def load(k, part):
        lo, n = ((0, 24), (24, rows - 24))[part]
        return pltpu.make_async_copy(
            field.at[:, lo:lo + n, pl.ds(pl.multiple_of(k * 128, 128), 128)],
            vol.at[:, k + 1, 8 + lo:8 + lo + n, :],
            load_sem.at[part, k],
        )

    for part in range(2):
        def start_load(k, _, part=part):
            load(k, part).start()
            return 0
        lax.fori_loop(0, blocks, start_load, 0)

    def clear(p, _):
        vol[p, 0, 8:8 + rows, :] = jnp.zeros((rows, 128), jnp.float32)
        vol[p, blocks + 1, 8:8 + rows, :] = jnp.zeros((rows, 128), jnp.float32)
        return 0

    lax.fori_loop(0, vol.shape[0], clear, 0)

    def clear_row(at):
        def step(p, _):
            vol[p, 1:blocks + 1, at:at + 1, :] = jnp.zeros((blocks, 1, 128), jnp.float32)
            return 0
        lax.fori_loop(0, vol.shape[0], step, 0)

    @pl.when(row_part == 0)
    def _():
        clear_row(7)

    @pl.when(row_part == narrow - 1)
    def _():
        clear_row(8 + rows)

    for b in range(wide):
        for o in range(wide):
            front[b * wide + o] = jnp.where(rank[o] < rank[b], 1.0, 0.0)

    light = [0.5 * light_dir[i] for i in range(3)]
    trans = [[-LOG2E * transfer[i, c] for c in range(3)] for i in range(2)]

    def wait_load(part):
        lo, n = ((0, 24), (24, rows - 24))[part]
        for k in range(blocks):
            load(k, part).wait()

    def compute(chunk):
        row = 8 + 8 * chunk

        def step(k, _):
            acc, depth = brick_cells(vol, k + 1, row, scale, light, trans)
            for c in range(3):
                send[chunk, k, c] = acc[c] * 0.5
            send[chunk, k, 3] = depth * scale
            return 0

        lax.fori_loop(0, blocks, step, 0)

    def block_copy(chunk, dy, dz, dc):
        return pltpu.make_async_remote_copy(
            src_ref=send.at[chunk, column_block(dy, dz, dc)],
            dst_ref=recv.at[chunk, me],
            send_sem=send_sem.at[chunk],
            recv_sem=recv_sem.at[chunk],
            device_id=(device(dy, dz, dc), row_part),
            device_id_type=MESH,
        )

    def send_chunk(chunk):
        for partner in PARTNERS:
            block_copy(chunk, *partner).start()

    def all_of(chunk):
        part = recv.at[chunk, 0:wide - 1]
        return pltpu.make_async_remote_copy(
            src_ref=send.at[chunk, 0:wide - 1], dst_ref=part, send_sem=send_sem.at[chunk], recv_sem=recv_sem.at[chunk],
            device_id=(device(1, 0, 0), row_part), device_id_type=MESH,
        )

    def composite(chunk):
        recv[chunk, me] = send[chunk, mine]
        all_of(chunk).wait_recv()
        depths = [recv[chunk, b, 3] for b in range(wide)]
        total = depths[0]
        for b in range(1, wide):
            total = total + depths[b]
        back = BACKGROUND * jnp.exp(-total)
        acc = [back] * 3
        for b in range(wide):
            ahead = jnp.zeros((8, 128), jnp.float32)
            for o in range(wide):
                if o != b:
                    ahead = ahead + front[b * wide + o] * depths[o]
            seen = jnp.exp(-ahead)
            for c in range(3):
                acc[c] = acc[c] + seen * recv[chunk, b, c]
        for c in range(3):
            image[c, chunk * 8:chunk * 8 + 8, pl.ds(pl.multiple_of(mine * 128, 128), 128)] = acc[c]

    def tile(chunk, start, count):
        return image.at[:, chunk * 8:chunk * 8 + 8, pl.ds(pl.multiple_of(start * 128, 128), count * 128)]

    def gather_copy(chunk, slot, start, count, dy, dz, dc, got):
        def made(at):
            return pltpu.make_async_remote_copy(
                src_ref=tile(chunk, at, count), dst_ref=tile(chunk, at, count),
                send_sem=ag_ssem.at[chunk, slot], recv_sem=ag_rsem.at[chunk, slot],
                device_id=(device(dy, dz, dc), row_part), device_id_type=MESH,
            )
        return functools.partial(made, start), functools.partial(made, got)

    def pair(dz):
        return core * 8 + ((z + dz) % 4) * 2

    def stage1(chunk):
        return [gather_copy(chunk, 0, mine, 1, 1, 0, 0, column_block(1, 0, 0))]

    def stage2(chunk):
        return [
            gather_copy(chunk, 1, pair(0), 2, 0, 1, 0, pair(3)),
            gather_copy(chunk, 2, pair(0), 2, 0, 3, 0, pair(1)),
        ]

    def stage3(chunk):
        return [
            gather_copy(chunk, 3, pair(3), 1, 0, 1, 0, pair(2)),
            gather_copy(chunk, 4, pair(1) + 1, 1, 0, 3, 0, pair(2) + 1),
        ]

    def stage4(chunk):
        return [gather_copy(chunk, 7, core * 8, 8, 0, 0, 1, ((core + 1) % 2) * 8)]

    def spread(chunk):
        return [
            gather_copy(chunk, i, mine, 1, dy, dz, 0, column_block(dy, 4 - dz, 0))
            for i, (dy, dz, dc) in enumerate(PARTNERS) if dc == 0
        ]

    order = list(range(1, chunks - 1)) + [0, chunks - 1]
    stages = {
        chunk: (stage1, stage2, stage3, stage4) if at < chunks - DIRECT else (spread, stage4)
        for at, chunk in enumerate(order)
    }

    def begin(stage, chunk):
        for sent, _ in stages[chunk][stage](chunk):
            sent().start()

    def end(stage, chunk):
        for _, got in stages[chunk][stage](chunk):
            got().wait_recv()

    def write(chunk):
        return pltpu.make_async_copy(
            image.at[:, chunk * 8:chunk * 8 + 8, :], out.at[:, chunk * 8:chunk * 8 + 8, :], out_sem.at[chunk]
        )

    def halo_up():
        return pltpu.make_async_remote_copy(
            src_ref=vol.at[:, 1:blocks + 1, 8:9, :], dst_ref=vol.at[:, 1:blocks + 1, 8 + rows:9 + rows, :],
            send_sem=halo_ssem.at[0], recv_sem=halo_rsem.at[0],
            device_id=(me, row_part - 1), device_id_type=MESH,
        )

    def halo_down():
        return pltpu.make_async_remote_copy(
            src_ref=vol.at[:, 1:blocks + 1, 7 + rows:8 + rows, :], dst_ref=vol.at[:, 1:blocks + 1, 7:8, :],
            send_sem=halo_ssem.at[1], recv_sem=halo_rsem.at[1],
            device_id=(me, row_part + 1), device_id_type=MESH,
        )

    has_up, has_down = row_part > 0, row_part < narrow - 1
    last = chunks + LAG + 4 * GAP
    for step in range(last):
        if step == 0:
            wait_load(0)
        if step < chunks:
            chunk = order[step]
            if chunk == 0:
                @pl.when(has_up)
                def _():
                    halo_down().wait_recv()
            if chunk == chunks - 1:
                @pl.when(has_down)
                def _():
                    halo_up().wait_recv()
            compute(chunk)
        if step == 0:
            wait_load(1)
            pl.semaphore_wait(barrier, wide - 1 + has_up.astype(jnp.int32) + has_down.astype(jnp.int32))

            @pl.when(has_up)
            def _():
                halo_up().start()

            @pl.when(has_down)
            def _():
                halo_down().start()
        if step < chunks:
            send_chunk(order[step])
        for at in range(chunks):
            chunk = order[at]
            count = len(stages[chunk])
            stage, rest = divmod(step - LAG - at, GAP)
            if rest or not 0 <= stage <= count:
                continue
            if stage == 0:
                composite(chunk)
            else:
                end(stage - 1, chunk)
            if stage < count:
                begin(stage, chunk)
            else:
                write(chunk).start()

    for chunk in range(chunks):
        all_of(chunk).wait_send()
        for stage in stages[chunk]:
            for sent, _ in stage(chunk):
                sent().wait_send()
        write(chunk).wait()

    @pl.when(has_up)
    def _():
        halo_up().wait_send()

    @pl.when(has_down)
    def _():
        halo_down().wait_send()


def solution(mesh):
    wide, narrow = mesh.shape["wide"], mesh.shape["narrow"]

    def body(scalar_field, depth_rank, transfer, light_dir):
        planes, rows, columns = scalar_field.shape
        blocks = columns // 128
        chunks = rows // 8
        scale = 2.0 / (planes * wide)
        smem = pl.BlockSpec(memory_space=pltpu.SMEM)
        return pl.pallas_call(
            functools.partial(kernel, (wide, narrow, rows, scale)),
            out_shape=jax.ShapeDtypeStruct((3, rows, columns), jnp.float32),
            in_specs=[pl.BlockSpec(memory_space=pl.ANY), smem, smem, smem],
            out_specs=pl.BlockSpec(memory_space=pl.ANY),
            scratch_shapes=[
                pltpu.VMEM((planes, blocks + 2, rows + 16, 128), jnp.float32),
                pltpu.VMEM((chunks, blocks, 4, 8, 128), jnp.float32),
                pltpu.VMEM((chunks, wide, 4, 8, 128), jnp.float32),
                pltpu.VMEM((3, rows, columns), jnp.float32),
                pltpu.SMEM((wide * wide,), jnp.float32),
                pltpu.SemaphoreType.DMA((2, blocks)),
                pltpu.SemaphoreType.DMA((2,)),
                pltpu.SemaphoreType.DMA((2,)),
                pltpu.SemaphoreType.DMA((chunks,)),
                pltpu.SemaphoreType.DMA((chunks,)),
                pltpu.SemaphoreType.DMA((chunks, 8)),
                pltpu.SemaphoreType.DMA((chunks, 8)),
                pltpu.SemaphoreType.DMA((chunks,)),
            ],
            compiler_params=pltpu.CompilerParams(collective_id=0, has_side_effects=True),
        )(scalar_field, depth_rank, transfer, light_dir)

    return jax.shard_map(
        body,
        mesh=mesh,
        in_specs=(P("wide", "narrow", None), P(), P(), P()),
        out_specs=P(None, "narrow", None),
        check_vma=False,
    )
```

```python
import functools
import math

import jax
import jax.numpy as jnp
from jax import lax
from jax.experimental import pallas as pl
from jax.experimental.pallas import tpu as pltpu
from jax.sharding import PartitionSpec as P

MESH = pl.DeviceIdType.MESH
BACKGROUND = 0.25
LOG2E = math.log2(math.e)
LAG = 3
GAP = 3
DIRECT = 4
PARTNERS = (
    (1, 2, 0), (1, 2, 1), (0, 2, 0), (0, 2, 1), (1, 1, 0), (1, 3, 1), (1, 3, 0), (1, 1, 1),
    (1, 0, 0), (0, 1, 0), (0, 3, 1), (0, 3, 0), (0, 1, 1), (1, 0, 1),
    (0, 0, 1),
)


def brick_cells(vol, tile, row, scale, light, trans):
    planes = vol.shape[0]
    lane = lax.broadcasted_iota(jnp.int32, (8, 128), 1)
    first, last = lane == 0, lane == 127
    zero = jnp.zeros((8, 128), jnp.float32)
    depth, through = zero, zero + 1.0
    acc = [zero] * 3
    value = vol[0, tile, pl.ds(row, 8), :]
    before = value
    for p in range(planes):
        after = vol[p + 1, tile, pl.ds(row, 8), :] if p + 1 < planes else value
        up = vol[p, tile, pl.ds(row - 1, 8), :]
        down = vol[p, tile, pl.ds(row + 1, 8), :]
        right = pltpu.roll(jnp.where(first, vol[p, tile + 1, pl.ds(row, 8), :], value), 127, 1)
        left = pltpu.roll(jnp.where(last, vol[p, tile - 1, pl.ds(row, 8), :], value), 1, 1)
        slope = light[0] * (after - before) + light[1] * (down - up) + light[2] * (right - left)
        depth = depth + jnp.log(1.0 + jnp.exp2(value * (2.0 * LOG2E)))
        beyond = jnp.exp2(depth * (-scale * LOG2E))
        weight = through - beyond
        through = beyond
        shaded = weight + weight * jnp.tanh(slope)
        den = [1.0 + jnp.exp2(trans[0][c] * value + trans[1][c]) for c in range(3)]
        den01 = den[0] * den[1]
        part = shaded / (den01 * den[2])
        part2 = part * den[2]
        acc[0] = acc[0] + part2 * den[1]
        acc[1] = acc[1] + part2 * den[0]
        acc[2] = acc[2] + part * den01
        before, value = value, after
    return acc, depth


def kernel(
    sizes, field, rank, transfer, light_dir, out,
    vol, send, recv, image, front,
    load_sem, halo_ssem, halo_rsem, send_sem, recv_sem, ag_ssem, ag_rsem, out_sem,
):
    wide, narrow, rows, scale = sizes
    blocks = wide
    chunks = rows // 8
    me = lax.axis_index("wide")
    row_part = lax.axis_index("narrow")
    y, z, core = me // 8, (me // 2) % 4, me % 2

    def device(dy, dz, dc):
        return ((y + dy) % 2) * 8 + ((z + dz) % 4) * 2 + (core + dc) % 2

    def column_block(dy, dz, dc):
        return ((core + dc) % 2) * 8 + ((z + dz) % 4) * 2 + (y + dy) % 2

    mine = column_block(0, 0, 0)

    barrier = pltpu.get_barrier_semaphore()
    for dy, dz, dc in PARTNERS:
        pl.semaphore_signal(barrier, inc=1, device_id=(device(dy, dz, dc), row_part), device_id_type=MESH)

    @pl.when(row_part > 0)
    def _():
        pl.semaphore_signal(barrier, inc=1, device_id=(me, row_part - 1), device_id_type=MESH)

    @pl.when(row_part < narrow - 1)
    def _():
        pl.semaphore_signal(barrier, inc=1, device_id=(me, row_part + 1), device_id_type=MESH)

    def load(k, part):
        lo, n = ((0, 24), (24, rows - 24))[part]
        return pltpu.make_async_copy(
            field.at[:, lo:lo + n, pl.ds(pl.multiple_of(k * 128, 128), 128)],
            vol.at[:, k + 1, 8 + lo:8 + lo + n, :],
            load_sem.at[part, k],
        )

    for part in range(2):
        def start_load(k, _, part=part):
            load(k, part).start()
            return 0
        lax.fori_loop(0, blocks, start_load, 0)

    def clear(p, _):
        vol[p, 0, 8:8 + rows, :] = jnp.zeros((rows, 128), jnp.float32)
        vol[p, blocks + 1, 8:8 + rows, :] = jnp.zeros((rows, 128), jnp.float32)
        return 0

    lax.fori_loop(0, vol.shape[0], clear, 0)

    def clear_row(at):
        def step(p, _):
            vol[p, 1:blocks + 1, at:at + 1, :] = jnp.zeros((blocks, 1, 128), jnp.float32)
            return 0
        lax.fori_loop(0, vol.shape[0], step, 0)

    @pl.when(row_part == 0)
    def _():
        clear_row(7)

    @pl.when(row_part == narrow - 1)
    def _():
        clear_row(8 + rows)

    for b in range(wide):
        for o in range(wide):
            front[b * wide + o] = jnp.where(rank[o] < rank[b], 1.0, 0.0)

    light = [0.5 * light_dir[i] for i in range(3)]
    trans = [[-LOG2E * transfer[i, c] for c in range(3)] for i in range(2)]

    def wait_load(part):
        lo, n = ((0, 24), (24, rows - 24))[part]
        for k in range(blocks):
            load(k, part).wait()

    def compute(chunk):
        row = 8 + 8 * chunk

        def step(k, _):
            acc, depth = brick_cells(vol, k + 1, row, scale, light, trans)
            for c in range(3):
                send[chunk, k, c] = acc[c] * 0.5
            send[chunk, k, 3] = depth * scale
            return 0

        lax.fori_loop(0, blocks, step, 0)

    def block_copy(chunk, dy, dz, dc):
        return pltpu.make_async_remote_copy(
            src_ref=send.at[chunk, column_block(dy, dz, dc)],
            dst_ref=recv.at[chunk, me],
            send_sem=send_sem.at[chunk],
            recv_sem=recv_sem.at[chunk],
            device_id=(device(dy, dz, dc), row_part),
            device_id_type=MESH,
        )

    def send_chunk(chunk):
        for partner in PARTNERS:
            block_copy(chunk, *partner).start()

    def all_of(chunk):
        part = recv.at[chunk, 0:wide - 1]
        return pltpu.make_async_remote_copy(
            src_ref=send.at[chunk, 0:wide - 1], dst_ref=part, send_sem=send_sem.at[chunk], recv_sem=recv_sem.at[chunk],
            device_id=(device(1, 0, 0), row_part), device_id_type=MESH,
        )

    def composite(chunk):
        recv[chunk, me] = send[chunk, mine]
        all_of(chunk).wait_recv()
        depths = [recv[chunk, b, 3] for b in range(wide)]
        total = depths[0]
        for b in range(1, wide):
            total = total + depths[b]
        back = BACKGROUND * jnp.exp(-total)
        acc = [back] * 3
        for b in range(wide):
            ahead = jnp.zeros((8, 128), jnp.float32)
            for o in range(wide):
                if o != b:
                    ahead = ahead + front[b * wide + o] * depths[o]
            seen = jnp.exp(-ahead)
            for c in range(3):
                acc[c] = acc[c] + seen * recv[chunk, b, c]
        for c in range(3):
            image[c, chunk * 8:chunk * 8 + 8, pl.ds(pl.multiple_of(mine * 128, 128), 128)] = acc[c]

    def tile(chunk, start, count):
        return image.at[:, chunk * 8:chunk * 8 + 8, pl.ds(pl.multiple_of(start * 128, 128), count * 128)]

    def gather_copy(chunk, slot, start, count, dy, dz, dc, got):
        def made(at):
            return pltpu.make_async_remote_copy(
                src_ref=tile(chunk, at, count), dst_ref=tile(chunk, at, count),
                send_sem=ag_ssem.at[chunk, slot], recv_sem=ag_rsem.at[chunk, slot],
                device_id=(device(dy, dz, dc), row_part), device_id_type=MESH,
            )
        return functools.partial(made, start), functools.partial(made, got)

    def pair(dz):
        return core * 8 + ((z + dz) % 4) * 2

    def stage1(chunk):
        return [gather_copy(chunk, 0, mine, 1, 1, 0, 0, column_block(1, 0, 0))]

    def stage2(chunk):
        return [
            gather_copy(chunk, 1, pair(0), 2, 0, 1, 0, pair(3)),
            gather_copy(chunk, 2, pair(0), 2, 0, 3, 0, pair(1)),
        ]

    def stage3(chunk):
        return [
            gather_copy(chunk, 3, pair(3), 1, 0, 1, 0, pair(2)),
            gather_copy(chunk, 4, pair(1) + 1, 1, 0, 3, 0, pair(2) + 1),
        ]

    def stage4(chunk):
        return [gather_copy(chunk, 7, core * 8, 8, 0, 0, 1, ((core + 1) % 2) * 8)]

    def spread(chunk):
        return [
            gather_copy(chunk, i, mine, 1, dy, dz, 0, column_block(dy, 4 - dz, 0))
            for i, (dy, dz) in enumerate([partner[:2] for partner in PARTNERS if partner[2] == 0])
        ]

    order = list(range(1, chunks - 1)) + [0, chunks - 1]
    stages = {
        chunk: (stage1, stage2, stage3, stage4) if at < chunks - DIRECT else (spread, stage4)
        for at, chunk in enumerate(order)
    }

    def begin(stage, chunk):
        for sent, _ in stages[chunk][stage](chunk):
            sent().start()

    def end(stage, chunk):
        for _, got in stages[chunk][stage](chunk):
            got().wait_recv()

    def write(chunk):
        return pltpu.make_async_copy(
            image.at[:, chunk * 8:chunk * 8 + 8, :], out.at[:, chunk * 8:chunk * 8 + 8, :], out_sem.at[chunk]
        )

    def halo_up():
        return pltpu.make_async_remote_copy(
            src_ref=vol.at[:, 1:blocks + 1, 8:9, :], dst_ref=vol.at[:, 1:blocks + 1, 8 + rows:9 + rows, :],
            send_sem=halo_ssem.at[0], recv_sem=halo_rsem.at[0],
            device_id=(me, row_part - 1), device_id_type=MESH,
        )

    def halo_down():
        return pltpu.make_async_remote_copy(
            src_ref=vol.at[:, 1:blocks + 1, 7 + rows:8 + rows, :], dst_ref=vol.at[:, 1:blocks + 1, 7:8, :],
            send_sem=halo_ssem.at[1], recv_sem=halo_rsem.at[1],
            device_id=(me, row_part + 1), device_id_type=MESH,
        )

    has_up, has_down = row_part > 0, row_part < narrow - 1
    last = chunks + LAG + 4 * GAP
    for step in range(last):
        if step == 0:
            wait_load(0)
        if step < chunks:
            chunk = order[step]
            if chunk == 0:
                @pl.when(has_up)
                def _():
                    halo_down().wait_recv()
            if chunk == chunks - 1:
                @pl.when(has_down)
                def _():
                    halo_up().wait_recv()
            compute(chunk)
        if step == 0:
            pl.semaphore_wait(barrier, wide - 1 + has_up.astype(jnp.int32) + has_down.astype(jnp.int32))
        if step < chunks:
            send_chunk(order[step])
        if step == 0:
            wait_load(1)
        if step == 1:
            @pl.when(has_up)
            def _():
                halo_up().start()

            @pl.when(has_down)
            def _():
                halo_down().start()

        for at in range(chunks):
            chunk = order[at]
            count = len(stages[chunk])
            stage, rest = divmod(step - LAG - at, GAP)
            if rest or not 0 <= stage <= count:
                continue
            if stage == 0:
                composite(chunk)
            else:
                end(stage - 1, chunk)
            if stage < count:
                begin(stage, chunk)
            else:
                write(chunk).start()

    for chunk in range(chunks):
        all_of(chunk).wait_send()
        for stage in stages[chunk]:
            for sent, _ in stage(chunk):
                sent().wait_send()
        write(chunk).wait()

    @pl.when(has_up)
    def _():
        halo_up().wait_send()

    @pl.when(has_down)
    def _():
        halo_down().wait_send()


def solution(mesh):
    wide, narrow = mesh.shape["wide"], mesh.shape["narrow"]

    def body(scalar_field, depth_rank, transfer, light_dir):
        planes, rows, columns = scalar_field.shape
        blocks = columns // 128
        chunks = rows // 8
        scale = 2.0 / (planes * wide)
        smem = pl.BlockSpec(memory_space=pltpu.SMEM)
        return pl.pallas_call(
            functools.partial(kernel, (wide, narrow, rows, scale)),
            out_shape=jax.ShapeDtypeStruct((3, rows, columns), jnp.float32),
            in_specs=[pl.BlockSpec(memory_space=pl.ANY), smem, smem, smem],
            out_specs=pl.BlockSpec(memory_space=pl.ANY),
            scratch_shapes=[
                pltpu.VMEM((planes, blocks + 2, rows + 16, 128), jnp.float32),
                pltpu.VMEM((chunks, blocks, 4, 8, 128), jnp.float32),
                pltpu.VMEM((chunks, wide, 4, 8, 128), jnp.float32),
                pltpu.VMEM((3, rows, columns), jnp.float32),
                pltpu.SMEM((wide * wide,), jnp.float32),
                pltpu.SemaphoreType.DMA((2, blocks)),
                pltpu.SemaphoreType.DMA((2,)),
                pltpu.SemaphoreType.DMA((2,)),
                pltpu.SemaphoreType.DMA((chunks,)),
                pltpu.SemaphoreType.DMA((chunks,)),
                pltpu.SemaphoreType.DMA((chunks, 8)),
                pltpu.SemaphoreType.DMA((chunks, 8)),
                pltpu.SemaphoreType.DMA((chunks,)),
            ],
            compiler_params=pltpu.CompilerParams(collective_id=0, has_side_effects=True),
        )(scalar_field, depth_rank, transfer, light_dir)

    return jax.shard_map(
        body,
        mesh=mesh,
        in_specs=(P("wide", "narrow", None), P(), P(), P()),
        out_specs=P(None, "narrow", None),
        check_vma=False,
    )
```
